32 devices in a mesh: gx: 4 (over x, core), gy: 8 (over z, y).
Axes of the slice: x: 2, y: 2, z: 4, core: 2. Of those that a mesh axis runs over, the one named last changes fastest.
Arguments:
- loads: bfloat16 [4, 8, 1024, 128], P('gx', 'gy'), may hold values from -6 to 6
- initial_guess: float32 [4, 8, 1024, 128], P('gx', 'gy'), may hold values from -3 to 3
- local_inverse: bfloat16 [4, 8, 1024, 1024], P('gx', 'gy'), may hold values from -0.25 to 1.25
- diag_coef: float32 [4, 8, 1024], P('gx', 'gy'), may hold values from 1 to 4
- couplings: float32 [4, 8, 1024], P('gx', 'gy'), may hold values from 0.2 to 0.6
- interface_rows: int32 [4, 8, 1024], P('gx', 'gy'), may hold values from 0 to 1023, each once within a row
- owned_mask: int32 [4, 8, 1024], P('gx', 'gy'), may hold values 0 or 1
- coarse_modes: float32 [4, 8, 1024, 6], P('gx', 'gy'), may hold values from -0.125 to 0.125
- coarse_inverse: bfloat16 [192, 192], P(('gx', 'gy')), may hold values from -0.875 to 0.875
Outputs:
- solution: float32 [4, 8, 1024, 128], P('gx', 'gy')
The draws below stay inside these ranges and needn't reach their ends.
All inputs are finite; a program needn't handle non-finite values. No bound on the sum of `owned_mask` on one device may be relied on, other than what follows from the above.
Results may differ from the reference program's by a relative error of at most 0.0033.
Values may be sent and summed in bfloat16 or wider, within the bound.
A program may use at most 64 MiB of HBM per device.

```python
import jax
import jax.numpy as jnp
from jax import lax

M = 1024
IR = 128
NM = 6
K = 128
ITERS = 1
SX = 4
SY = 8
NC = 192


def diagonal_values(key):
    uniform_part = jax.random.uniform(jax.random.fold_in(key, 11), (SX, SY, M), jnp.float32)
    return jnp.exp(uniform_part * jnp.log(4.0))


def draw_diag_coef(key, part):
    return diagonal_values(key)


def draw_local_inverse(key, part):
    scaling = diagonal_values(key)
    noise_key = jax.random.fold_in(key, 23)
    noise = jnp.clip(jax.random.normal(noise_key, (SX, SY, M, M), jnp.float32), -4.0, 4.0)
    identity = jnp.eye(M, dtype=jnp.float32)
    matrix = (identity + 0.3 / jnp.sqrt(float(M)) * noise) / scaling[..., :, None]
    return matrix.astype(jnp.bfloat16)


def touch_ends(values, rng, smallest, high):
    spot = [jax.random.randint(jax.random.fold_in(rng, axis), (), 0, length) for axis, length in enumerate(values.shape)]
    main_axis = values.shape.index(max(values.shape))
    neighbour = spot[:main_axis] + [(spot[main_axis] + 1) % values.shape[main_axis]] + spot[main_axis + 1:]
    return values.at[tuple(spot)].set(smallest).at[tuple(neighbour)].set(high)


def strengthened(values, key, source, target, parts, factor):
    def block_of(position):
        return (jnp.arange(values.shape[position]) // (values.shape[position] // parts)).reshape((-1,) + (1,) * (values.ndim - 1 - position))

    one_side = jax.random.permutation(key, parts)[block_of(target)]
    second = (block_of(target) + parts // 2) % parts
    return jnp.where((block_of(source) == one_side) | (block_of(source) == second), factor * values, values)


def block_scale(own_key, extent, shards, least, top_value):
    def one(axis_at, shards_of):
        draws = jax.random.uniform(jax.random.fold_in(jax.random.fold_in(own_key, 6), axis_at), (shards_of,), jnp.float32, least / len(shards), top_value / len(shards))
        return jnp.repeat(jnp.exp(draws), extent[axis_at] // shards_of).reshape((-1,) + (1,) * (len(extent) - axis_at - 1))

    gain = one(*shards[0])
    for cut in shards[1:]:
        gain = gain * one(*cut)
    return gain


def scatter_about(stream_key, extent, scale, reach, cuts=(), kind=jnp.bfloat16):
    result = jax.random.normal(stream_key, extent, jnp.float32) * scale
    if len(cuts) > 0:
        result = block_scale(stream_key, extent, cuts, -0.22, 0.18) * result
    return jnp.clip(result, min=-reach, max=reach).astype(kind)


def bell_draw_with(rng, dims, width, bound, split, heavy, kind=jnp.bfloat16):
    entries = width * jax.random.normal(rng, dims, jnp.float32)
    if split:
        entries = entries * block_scale(rng, dims, split, -0.22, 0.18)
    return jnp.clip(strengthened(entries, jax.random.fold_in(rng, 3), *heavy), -bound, bound).astype(kind)


def setup_inputs(seed: int = 0) -> dict:
    keys = jax.random.split(jax.random.key(seed), 10)
    loads = scatter_about(keys[0], (SX, SY, M, K), 1.0, 6.0, ((0, 4), (1, 8)))
    initial_guess = scatter_about(keys[1], (SX, SY, M, K), 0.5, 3.0, ((0, 4), (1, 8)), jnp.float32)
    local_inverse = draw_local_inverse(jax.random.fold_in(keys[9], 71), 0)
    diag_coef = draw_diag_coef(jax.random.fold_in(keys[9], 71), 0)
    couplings = jnp.clip(0.2 + 0.400000021 * jax.random.uniform(keys[4], (SX, SY, M), jnp.float32) ** block_scale(keys[4], (SX, SY, M), ((0, 4), (1, 8)), -0.2, 0.2), 0.2, 0.6)
    interface_rows = jax.vmap(lambda own: jax.random.permutation(own, M))(jax.random.split(keys[5], SX * SY)).reshape((SX, SY, M)).astype(jnp.int32)
    owned_mask = touch_ends((jax.random.randint(keys[6], (SX, SY, M), 0, 4) < 3).astype(jnp.int32), jax.random.fold_in(keys[6], 1), 0, 1)
    coarse_modes = scatter_about(keys[7], (SX, SY, M, NM), (2 * M) ** -0.5, 0.125, ((0, 4), (1, 8)), jnp.float32)
    coarse_inverse = bell_draw_with(keys[8], (NC, NC), NC ** -0.5, 0.875, ((0, 32),), (1, 0, 32, 2.75))
    return dict(loads=loads, initial_guess=initial_guess, local_inverse=local_inverse, diag_coef=diag_coef, couplings=couplings, interface_rows=interface_rows, owned_mask=owned_mask, coarse_modes=coarse_modes, coarse_inverse=coarse_inverse)


def place_rows(row_order, values):
    return jnp.zeros((M, values.shape[1]), jnp.float32).at[row_order].set(values)


def apply_operator(field, diag_coef, couplings, interface_rows):
    side_order = interface_rows[..., :4 * IR]
    gathered = jnp.take_along_axis(field, side_order[..., None], axis=2)
    sides = gathered.reshape(SX, SY, 4, IR, K)
    zero_x = jnp.zeros_like(sides[:1, :, 0])
    from_below = jnp.concatenate([zero_x, sides[:-1, :, 1]], 0)
    from_above = jnp.concatenate([sides[1:, :, 0], zero_x], 0)
    zero_y = jnp.zeros_like(sides[:, :1, 0])
    from_left = jnp.concatenate([zero_y, sides[:, :-1, 3]], 1)
    from_right = jnp.concatenate([sides[:, 1:, 2], zero_y], 1)
    received = jnp.concatenate([from_below, from_above, from_left, from_right], 2)
    placed = jax.vmap(jax.vmap(place_rows))(side_order, received)
    return diag_coef[..., None] * field - couplings[..., None] * placed


def local_products(local_inverse, residual_half):
    flat_inverse = local_inverse.reshape(SX * SY, M, M)
    flat_residual = residual_half.reshape(SX * SY, M, K)

    def one_solve(pair):
        return jnp.dot(pair[0], pair[1], preferred_element_type=jnp.float32)

    return lax.map(one_solve, (flat_inverse, flat_residual)).reshape(SX, SY, M, K)


def reference(loads, initial_guess, local_inverse, diag_coef, couplings, interface_rows, owned_mask, coarse_modes, coarse_inverse):
    load_values = loads.astype(jnp.float32)
    owned = owned_mask.astype(jnp.float32)[..., None]
    solution = initial_guess
    for iteration in range(ITERS):
        residual = load_values - apply_operator(solution, diag_coef, couplings, interface_rows)
        residual_half = residual.astype(jnp.bfloat16)
        local_step = owned * local_products(local_inverse, residual_half)
        coarse_res = jnp.einsum("xymc,xymk->xyck", coarse_modes, residual, precision=lax.Precision.HIGHEST).astype(jnp.bfloat16)
        coarse_coef = jnp.dot(coarse_inverse, coarse_res.reshape(NC, K), preferred_element_type=jnp.float32)
        coarse_coef = coarse_coef.reshape(SX, SY, NM, K)
        correction = jnp.einsum("xymc,xyck->xymk", coarse_modes, coarse_coef, precision=lax.Precision.HIGHEST)
        solution = solution + local_step + correction
    return solution
```

```python
import functools

import jax
import jax.numpy as jnp
from jax import lax
from jax.experimental import pallas as pl
from jax.experimental.pallas import tpu as pltpu
from jax.sharding import PartitionSpec as P

MESH = pl.DeviceIdType.MESH
LANES = 128
SLOT = 8


def one_hot(mask):
    return jnp.where(mask, 1.0, 0.0).astype(jnp.bfloat16)


def split(values):
    high = values.astype(jnp.bfloat16)
    return high, (values - high.astype(jnp.float32)).astype(jnp.bfloat16)


def peer_offsets(nx, ny):
    offsets = [(a, b) for a in range(nx) for b in range(ny) if a or b]
    return sorted(offsets, key=lambda o: abs(o[1] - ny // 2))


def for_each_peer(nx, ny, ix, iy, action):
    if nx * ny <= 64:
        for a, b in peer_offsets(nx, ny):
            action(lax.rem(ix + a, nx), lax.rem(iy + b, ny))
        return

    def step(offset, carry):
        action(lax.rem(ix + offset // ny, nx), lax.rem(iy + offset % ny, ny))
        return carry

    lax.fori_loop(1, nx * ny, step, 0)


def kernel(
    nx, ny, modes_count,
    loads_h, guess_h, inverse_h, diag_h, coup_h, rows_h, owned_h, modes_h, cinv_h,
    out_h,
    loads, guess, inverse, diag, coup, rows, owned, modes, cinv,
    halo_send, halo_recv, place, base, total, gathered, coarse_send, spread, lift,
    in_sem, halo_ssem, halo_rsem, coarse_ssem, coarse_rsem, out_sem,
):
    n = nx * ny
    m, k = guess.shape
    chunks = m // LANES
    ix, iy = lax.axis_index("gx"), lax.axis_index("gy")
    me = ix * ny + iy

    pairs = [
        (rows_h, rows), (guess_h, guess), (coup_h, coup), (modes_h, modes),
        (diag_h, diag), (loads_h, loads), (cinv_h, cinv), (owned_h, owned),
        (inverse_h, inverse),
    ]
    fetch = [pltpu.make_async_copy(a, b, in_sem.at[i]) for i, (a, b) in enumerate(pairs)]
    for copy in fetch:
        copy.start()
    barrier = pltpu.get_barrier_semaphore()
    for_each_peer(
        nx, ny, ix, iy,
        lambda px, py: pl.semaphore_signal(barrier, inc=1, device_id=(px, py), device_id_type=MESH),
    )

    fetch[0].wait()
    fetch[1].wait()
    guess_half = guess[...].astype(jnp.bfloat16)
    row_columns = rows[...].astype(jnp.float32).T
    lane = lax.broadcasted_iota(jnp.int32, (LANES, m), 1).astype(jnp.float32)
    for side in range(4):
        pick = one_hot(lane == row_columns[:, side : side + 1])
        values = jnp.dot(pick, guess_half, preferred_element_type=jnp.float32)
        halo_send[side] = values.astype(jnp.bfloat16)
    for side, edge in enumerate((ix == 0, ix == nx - 1, iy == 0, iy == ny - 1)):
        @pl.when(edge)
        def _():
            halo_recv[side] = jnp.zeros((LANES, k), jnp.bfloat16)

    pl.semaphore_wait(barrier, n - 1)

    sends = []
    for source, target, exists, dx, dy in (
        (3, 2, iy < ny - 1, 0, 1),
        (2, 3, iy > 0, 0, -1),
        (1, 0, ix < nx - 1, 1, 0),
        (0, 1, ix > 0, -1, 0),
    ):
        copy = pltpu.make_async_remote_copy(
            src_ref=halo_send.at[source],
            dst_ref=halo_recv.at[target],
            send_sem=halo_ssem.at[source],
            recv_sem=halo_rsem.at[target],
            device_id=(ix + dx, iy + dy),
            device_id_type=MESH,
        )
        sends.append((copy, exists))
        pl.when(exists)(copy.start)

    row_lanes = jnp.concatenate([rows[s : s + 1, :] for s in range(4)], axis=1)
    for j in range(chunks):
        sub = lax.broadcasted_iota(jnp.int32, (LANES, 4 * LANES), 0) + j * LANES
        place[j * LANES : (j + 1) * LANES, :] = one_hot(sub == row_lanes)
    fetch[2].wait()
    fetch[3].wait()
    zero_rows = jnp.zeros((SLOT - modes_count, LANES), jnp.float32)
    mode_rows = [
        jnp.concatenate([modes[c, :, j * LANES : (j + 1) * LANES] for c in range(modes_count)] + [zero_rows], axis=0)
        for j in range(chunks)
    ]
    scaled = jnp.concatenate([mode_rows[j] * coup[j : j + 1, :] for j in range(chunks)], axis=1)
    scaled = jnp.concatenate(split(scaled), axis=0)
    coarse_pick = jnp.dot(scaled, place[...], preferred_element_type=jnp.float32).astype(jnp.bfloat16)

    fetch[4].wait()
    fetch[5].wait()
    diag_columns = diag[...].T
    for j in range(chunks):
        at = pl.ds(j * LANES, LANES)
        base[at, :] = loads[at, :].astype(jnp.float32) - diag_columns[:, j : j + 1] * guess[at, :]
    coarse_base = jnp.dot(
        jnp.concatenate(mode_rows, axis=1), base[...],
        precision=lax.Precision.HIGHEST, preferred_element_type=jnp.float32,
    )

    fetch[6].wait()
    group = min(n, 64)
    narrow, wide = group * modes_count, group * SLOT
    wide_at = lax.broadcasted_iota(jnp.int32, (narrow, wide), 1)
    slot_row = lax.rem(wide_at, SLOT)
    source_row = lax.div(wide_at, SLOT) * modes_count + slot_row
    narrow_at = lax.broadcasted_iota(jnp.int32, (narrow, wide), 0)
    expand = one_hot((narrow_at == source_row) & (slot_row < modes_count))
    for g in range(n // group):
        spread[:, g * wide : (g + 1) * wide] = jnp.dot(
            cinv[:, g * narrow : (g + 1) * narrow], expand, preferred_element_type=jnp.float32
        ).astype(jnp.bfloat16)
    for j in range(chunks):
        high, low = split(mode_rows[j])
        high, low = high.astype(jnp.float32), low.astype(jnp.float32)
        stack = jnp.concatenate(
            [high, high, low, jnp.zeros((LANES - 3 * SLOT, LANES), jnp.float32)], axis=0
        )
        lift[j * LANES : (j + 1) * LANES, :] = stack.T.astype(jnp.bfloat16)

    for copy, exists in sends:
        pl.when(exists)(copy.wait_send)
    for side, exists in enumerate((ix > 0, ix < nx - 1, iy > 0, iy < ny - 1)):
        slot = halo_recv.at[side]
        arrival = pltpu.make_async_copy(slot, slot, halo_rsem.at[side])
        pl.when(exists)(arrival.wait)

    received = halo_recv[...].reshape(4 * LANES, k)
    terms = jnp.dot(coarse_pick, received, preferred_element_type=jnp.float32)
    coarse = (coarse_base + terms[:SLOT] + terms[SLOT:]).astype(jnp.bfloat16)
    coarse_send[...] = coarse
    gathered[pl.ds(me, 1)] = coarse[None]

    def send_coarse(px, py):
        pltpu.make_async_remote_copy(
            src_ref=coarse_send,
            dst_ref=gathered.at[me],
            send_sem=coarse_ssem,
            recv_sem=coarse_rsem,
            device_id=(px, py),
            device_id_type=MESH,
        ).start()

    for_each_peer(nx, ny, ix, iy, send_coarse)

    coup_columns = coup[...].T
    placed = jnp.dot(place[...], received, preferred_element_type=jnp.float32)
    residual_half = []
    for j in range(chunks):
        at = slice(j * LANES, (j + 1) * LANES)
        residual_half.append(
            (base[at, :] + coup_columns[:, j : j + 1] * placed[at]).astype(jnp.bfloat16)
        )
    residual_half = jnp.concatenate(residual_half, axis=0)
    fetch[7].wait()
    fetch[8].wait()
    owned_columns = owned[...].astype(jnp.float32).T
    for j in range(chunks):
        at = slice(j * LANES, (j + 1) * LANES)
        local = jnp.dot(inverse[at, :], residual_half, preferred_element_type=jnp.float32)
        total[at, :] = guess[at, :] + owned_columns[:, j : j + 1] * local

    everyone = gathered.at[pl.ds(0, n - 1)]
    pltpu.make_async_copy(everyone, everyone, coarse_ssem).wait()
    pltpu.make_async_copy(everyone, everyone, coarse_rsem).wait()

    coef = jnp.dot(
        spread[...], gathered[...].reshape(n * SLOT, k), preferred_element_type=jnp.float32
    )
    coef = jnp.concatenate([coef, jnp.zeros((SLOT - modes_count, k), jnp.float32)], axis=0)
    high, low = split(coef)
    stack = jnp.concatenate(
        [high, low, high, jnp.zeros((LANES - 3 * SLOT, k), jnp.bfloat16)], axis=0
    )
    stores = []
    for j in range(chunks):
        at = pl.ds(j * LANES, LANES)
        total[at, :] = total[at, :] + jnp.dot(
            lift[at, :], stack, preferred_element_type=jnp.float32
        )
        copy = pltpu.make_async_copy(total.at[at], out_h.at[at], out_sem.at[j])
        copy.start()
        stores.append(copy)
    for copy in stores:
        copy.wait()


def body(nx, ny, *args):
    loads, guess, inverse, diag, coup, rows, owned, modes, cinv = args
    m, k = guess.shape[2:]
    modes_count = modes.shape[3]
    n = nx * ny
    chunks = m // LANES
    small = (chunks, LANES)
    operands = (
        loads[0, 0], guess[0, 0], inverse[0, 0],
        diag.reshape(small), coup.reshape(small), rows.reshape(small), owned.reshape(small),
        jnp.transpose(modes[0], (2, 0, 1)), cinv,
    )
    scratch = [pltpu.VMEM(a.shape, a.dtype) for a in operands] + [
        pltpu.VMEM((4, LANES, k), jnp.bfloat16),
        pltpu.VMEM((4, LANES, k), jnp.bfloat16),
        pltpu.VMEM((m, 4 * LANES), jnp.bfloat16),
        pltpu.VMEM((m, k), jnp.float32),
        pltpu.VMEM((m, k), jnp.float32),
        pltpu.VMEM((n, SLOT, k), jnp.bfloat16),
        pltpu.VMEM((SLOT, k), jnp.bfloat16),
        pltpu.VMEM((modes_count, n * SLOT), jnp.bfloat16),
        pltpu.VMEM((m, LANES), jnp.bfloat16),
        pltpu.SemaphoreType.DMA((len(operands),)),
        pltpu.SemaphoreType.DMA((4,)),
        pltpu.SemaphoreType.DMA((4,)),
        pltpu.SemaphoreType.DMA,
        pltpu.SemaphoreType.DMA,
        pltpu.SemaphoreType.DMA((chunks,)),
    ]
    result = pl.pallas_call(
        functools.partial(kernel, nx, ny, modes_count),
        out_shape=jax.ShapeDtypeStruct((m, k), jnp.float32),
        in_specs=[pl.BlockSpec(memory_space=pl.ANY)] * len(operands),
        out_specs=pl.BlockSpec(memory_space=pl.ANY),
        scratch_shapes=scratch,
        compiler_params=pltpu.CompilerParams(collective_id=0, has_side_effects=True),
    )(*operands)
    return result[None, None]


def solution(mesh):
    nx, ny = mesh.shape["gx"], mesh.shape["gy"]
    return jax.shard_map(
        functools.partial(body, nx, ny),
        mesh=mesh,
        in_specs=(
            P("gx", "gy", None, None),
            P("gx", "gy", None, None),
            P("gx", "gy", None, None),
            P("gx", "gy", None),
            P("gx", "gy", None),
            P("gx", "gy", None),
            P("gx", "gy", None),
            P("gx", "gy", None, None),
            P(("gx", "gy"), None),
        ),
        out_specs=P("gx", "gy", None, None),
        check_vma=False,
    )
```

```python
import functools

import jax
import jax.numpy as jnp
from jax import lax
from jax.experimental import pallas as pl
from jax.experimental.pallas import tpu as pltpu
from jax.sharding import PartitionSpec as P

MESH = pl.DeviceIdType.MESH
LANES = 128
SLOT = 8


def one_hot(mask):
    return jnp.where(mask, 1.0, 0.0).astype(jnp.bfloat16)


def split(values):
    high = values.astype(jnp.bfloat16)
    return high, (values - high.astype(jnp.float32)).astype(jnp.bfloat16)


def peer_offsets(nx, ny):
    offsets = [(a, b) for a in range(nx) for b in range(ny) if a or b]
    return sorted(offsets, key=lambda o: abs(o[1] - ny // 2))


def for_each_peer(nx, ny, ix, iy, action):
    if nx * ny <= 64:
        for a, b in peer_offsets(nx, ny):
            action(lax.rem(ix + a, nx), lax.rem(iy + b, ny))
        return

    def step(offset, carry):
        action(lax.rem(ix + offset // ny, nx), lax.rem(iy + offset % ny, ny))
        return carry

    lax.fori_loop(1, nx * ny, step, 0)


def column_reaches(ny):
    reaches = [2]
    while 2 * reaches[-1] < ny - 1:
        reaches.append(2 * reaches[-1])
    return reaches


def greet_column(ny, ix, iy, semaphore, reach):
    for step in (reach, -reach):
        there = iy + step

        @pl.when((there >= 0) & (there < ny))
        def _():
            pl.semaphore_signal(semaphore, inc=1, device_id=(ix, there), device_id_type=MESH)

    return jnp.where(iy + reach < ny, 1, 0) + jnp.where(iy >= reach, 1, 0)


def greet_row(nx, ix, iy, semaphore):
    for step in range(1, nx):
        there = lax.rem(ix + step, nx)
        pl.semaphore_signal(semaphore, inc=1, device_id=(there, iy), device_id_type=MESH)
    return nx - 1


def kernel(
    nx, ny, modes_count,
    loads_h, guess_h, inverse_h, diag_h, coup_h, rows_h, owned_h, modes_h, cinv_h,
    out_h,
    loads, guess, inverse, diag, coup, rows, owned, modes, cinv,
    halo_send, halo_recv, place, base, total, gathered, coarse_send, spread, lift,
    in_sem, halo_ssem, halo_rsem, coarse_ssem, coarse_rsem, out_sem, ready,
):
    n = nx * ny
    m, k = guess.shape
    chunks = m // LANES
    ix, iy = lax.axis_index("gx"), lax.axis_index("gy")
    me = ix * ny + iy

    pairs = [
        (rows_h, rows), (guess_h, guess), (coup_h, coup), (modes_h, modes),
        (diag_h, diag), (loads_h, loads), (cinv_h, cinv), (owned_h, owned),
        (inverse_h, inverse),
    ]
    fetch = [pltpu.make_async_copy(a, b, in_sem.at[i]) for i, (a, b) in enumerate(pairs)]
    for copy in fetch:
        copy.start()
    barrier = pltpu.get_barrier_semaphore()
    greeted = greet_row(nx, ix, iy, barrier)
    greeted += greet_column(ny, ix, iy, barrier, 1) + greet_column(ny, ix, iy, barrier, 2)

    fetch[0].wait()
    fetch[1].wait()
    guess_half = guess[...].astype(jnp.bfloat16)
    row_columns = rows[...].astype(jnp.float32).T
    lane = lax.broadcasted_iota(jnp.int32, (LANES, m), 1).astype(jnp.float32)
    for side in range(4):
        pick = one_hot(lane == row_columns[:, side : side + 1])
        values = jnp.dot(pick, guess_half, preferred_element_type=jnp.float32)
        halo_send[side] = values.astype(jnp.bfloat16)
    for side, edge in enumerate((ix == 0, ix == nx - 1, iy == 0, iy == ny - 1)):
        @pl.when(edge)
        def _():
            halo_recv[side] = jnp.zeros((LANES, k), jnp.bfloat16)

    pl.semaphore_wait(barrier, greeted)

    sends = []
    for source, target, exists, dx, dy in (
        (3, 2, iy < ny - 1, 0, 1),
        (2, 3, iy > 0, 0, -1),
        (1, 0, ix < nx - 1, 1, 0),
        (0, 1, ix > 0, -1, 0),
    ):
        copy = pltpu.make_async_remote_copy(
            src_ref=halo_send.at[source],
            dst_ref=halo_recv.at[target],
            send_sem=halo_ssem.at[source],
            recv_sem=halo_rsem.at[target],
            device_id=(ix + dx, iy + dy),
            device_id_type=MESH,
        )
        sends.append((copy, exists))
        pl.when(exists)(copy.start)
    reaches = column_reaches(ny)
    expected = greet_column(ny, ix, iy, ready.at[0], reaches[0])

    row_lanes = jnp.concatenate([rows[s : s + 1, :] for s in range(4)], axis=1)
    for j in range(chunks):
        sub = lax.broadcasted_iota(jnp.int32, (LANES, 4 * LANES), 0) + j * LANES
        place[j * LANES : (j + 1) * LANES, :] = one_hot(sub == row_lanes)
    fetch[2].wait()
    fetch[3].wait()
    zero_rows = jnp.zeros((SLOT - modes_count, LANES), jnp.float32)
    mode_rows = [
        jnp.concatenate([modes[c, :, j * LANES : (j + 1) * LANES] for c in range(modes_count)] + [zero_rows], axis=0)
        for j in range(chunks)
    ]
    scaled = jnp.concatenate([mode_rows[j] * coup[j : j + 1, :] for j in range(chunks)], axis=1)
    scaled = jnp.concatenate(split(scaled), axis=0)
    coarse_pick = jnp.dot(scaled, place[...], preferred_element_type=jnp.float32).astype(jnp.bfloat16)

    def late_base():
        fetch[4].wait()
        fetch[5].wait()
        diag_columns = diag[...].T
        for j in range(chunks):
            at = pl.ds(j * LANES, LANES)
            base[at, :] = loads[at, :].astype(jnp.float32) - diag_columns[:, j : j + 1] * guess[at, :]

    for step, reach in enumerate(reaches):
        pl.semaphore_wait(ready.at[step], expected)
        if step + 1 < len(reaches):
            expected = greet_column(ny, ix, iy, ready.at[step + 1], reaches[step + 1])
        if step == 0:
            late_base()
    expected = greet_row(nx, ix, iy, ready.at[len(reaches)])
    coarse_base = jnp.dot(
        jnp.concatenate(mode_rows, axis=1), base[...],
        precision=lax.Precision.HIGHEST, preferred_element_type=jnp.float32,
    )

    fetch[6].wait()
    group = min(n, 64)
    narrow, wide = group * modes_count, group * SLOT
    wide_at = lax.broadcasted_iota(jnp.int32, (narrow, wide), 1)
    slot_row = lax.rem(wide_at, SLOT)
    source_row = lax.div(wide_at, SLOT) * modes_count + slot_row
    narrow_at = lax.broadcasted_iota(jnp.int32, (narrow, wide), 0)
    expand = one_hot((narrow_at == source_row) & (slot_row < modes_count))
    for g in range(n // group):
        spread[:, g * wide : (g + 1) * wide] = jnp.dot(
            cinv[:, g * narrow : (g + 1) * narrow], expand, preferred_element_type=jnp.float32
        ).astype(jnp.bfloat16)
    for j in range(chunks):
        high, low = split(mode_rows[j])
        high, low = high.astype(jnp.float32), low.astype(jnp.float32)
        stack = jnp.concatenate(
            [high, high, low, jnp.zeros((LANES - 3 * SLOT, LANES), jnp.float32)], axis=0
        )
        lift[j * LANES : (j + 1) * LANES, :] = stack.T.astype(jnp.bfloat16)

    pl.semaphore_wait(ready.at[len(reaches)], expected)
    for side, exists in enumerate((ix > 0, ix < nx - 1, iy > 0, iy < ny - 1)):
        slot = halo_recv.at[side]
        arrival = pltpu.make_async_copy(slot, slot, halo_rsem.at[side])
        pl.when(exists)(arrival.wait)

    received = halo_recv[...].reshape(4 * LANES, k)
    terms = jnp.dot(coarse_pick, received, preferred_element_type=jnp.float32)
    coarse = (coarse_base + terms[:SLOT] + terms[SLOT:]).astype(jnp.bfloat16)
    coarse_send[...] = coarse
    gathered[pl.ds(me, 1)] = coarse[None]

    def send_coarse(px, py):
        pltpu.make_async_remote_copy(
            src_ref=coarse_send,
            dst_ref=gathered.at[me],
            send_sem=coarse_ssem,
            recv_sem=coarse_rsem,
            device_id=(px, py),
            device_id_type=MESH,
        ).start()

    for_each_peer(nx, ny, ix, iy, send_coarse)

    coup_columns = coup[...].T
    placed = jnp.dot(place[...], received, preferred_element_type=jnp.float32)
    residual_half = []
    for j in range(chunks):
        at = slice(j * LANES, (j + 1) * LANES)
        residual_half.append(
            (base[at, :] + coup_columns[:, j : j + 1] * placed[at]).astype(jnp.bfloat16)
        )
    residual_half = jnp.concatenate(residual_half, axis=0)
    fetch[7].wait()
    fetch[8].wait()
    owned_columns = owned[...].astype(jnp.float32).T
    for j in range(chunks):
        at = slice(j * LANES, (j + 1) * LANES)
        local = jnp.dot(inverse[at, :], residual_half, preferred_element_type=jnp.float32)
        total[at, :] = guess[at, :] + owned_columns[:, j : j + 1] * local

    for copy, exists in sends:
        pl.when(exists)(copy.wait_send)
    everyone = gathered.at[pl.ds(0, n - 1)]
    pltpu.make_async_copy(everyone, everyone, coarse_ssem).wait()
    pltpu.make_async_copy(everyone, everyone, coarse_rsem).wait()

    coef = jnp.dot(
        spread[...], gathered[...].reshape(n * SLOT, k), preferred_element_type=jnp.float32
    )
    coef = jnp.concatenate([coef, jnp.zeros((SLOT - modes_count, k), jnp.float32)], axis=0)
    high, low = split(coef)
    stack = jnp.concatenate(
        [high, low, high, jnp.zeros((LANES - 3 * SLOT, k), jnp.bfloat16)], axis=0
    )
    stores = []
    for j in range(chunks):
        at = pl.ds(j * LANES, LANES)
        total[at, :] = total[at, :] + jnp.dot(
            lift[at, :], stack, preferred_element_type=jnp.float32
        )
        copy = pltpu.make_async_copy(total.at[at], out_h.at[at], out_sem.at[j])
        copy.start()
        stores.append(copy)
    for copy in stores:
        copy.wait()


def body(nx, ny, *args):
    loads, guess, inverse, diag, coup, rows, owned, modes, cinv = args
    m, k = guess.shape[2:]
    modes_count = modes.shape[3]
    n = nx * ny
    chunks = m // LANES
    small = (chunks, LANES)
    operands = (
        loads[0, 0], guess[0, 0], inverse[0, 0],
        diag.reshape(small), coup.reshape(small), rows.reshape(small), owned.reshape(small),
        jnp.transpose(modes[0], (2, 0, 1)), cinv,
    )
    scratch = [pltpu.VMEM(a.shape, a.dtype) for a in operands] + [
        pltpu.VMEM((4, LANES, k), jnp.bfloat16),
        pltpu.VMEM((4, LANES, k), jnp.bfloat16),
        pltpu.VMEM((m, 4 * LANES), jnp.bfloat16),
        pltpu.VMEM((m, k), jnp.float32),
        pltpu.VMEM((m, k), jnp.float32),
        pltpu.VMEM((n, SLOT, k), jnp.bfloat16),
        pltpu.VMEM((SLOT, k), jnp.bfloat16),
        pltpu.VMEM((modes_count, n * SLOT), jnp.bfloat16),
        pltpu.VMEM((m, LANES), jnp.bfloat16),
        pltpu.SemaphoreType.DMA((len(operands),)),
        pltpu.SemaphoreType.DMA((4,)),
        pltpu.SemaphoreType.DMA((4,)),
        pltpu.SemaphoreType.DMA,
        pltpu.SemaphoreType.DMA,
        pltpu.SemaphoreType.DMA((chunks,)),
        pltpu.SemaphoreType.REGULAR((len(column_reaches(ny)) + 1,)),
    ]
    result = pl.pallas_call(
        functools.partial(kernel, nx, ny, modes_count),
        out_shape=jax.ShapeDtypeStruct((m, k), jnp.float32),
        in_specs=[pl.BlockSpec(memory_space=pl.ANY)] * len(operands),
        out_specs=pl.BlockSpec(memory_space=pl.ANY),
        scratch_shapes=scratch,
        compiler_params=pltpu.CompilerParams(collective_id=0, has_side_effects=True),
    )(*operands)
    return result[None, None]


def solution(mesh):
    nx, ny = mesh.shape["gx"], mesh.shape["gy"]
    return jax.shard_map(
        functools.partial(body, nx, ny),
        mesh=mesh,
        in_specs=(
            P("gx", "gy", None, None),
            P("gx", "gy", None, None),
            P("gx", "gy", None, None),
            P("gx", "gy", None),
            P("gx", "gy", None),
            P("gx", "gy", None),
            P("gx", "gy", None),
            P("gx", "gy", None, None),
            P(("gx", "gy"), None),
        ),
        out_specs=P("gx", "gy", None, None),
        check_vma=False,
    )
```

```python
import functools

import jax
import jax.numpy as jnp
from jax import lax
from jax.experimental import pallas as pl
from jax.experimental.pallas import tpu as pltpu
from jax.sharding import PartitionSpec as P

MESH = pl.DeviceIdType.MESH
LANES = 128
SLOT = 8


def one_hot(mask):
    return jnp.where(mask, 1.0, 0.0).astype(jnp.bfloat16)


def split(values):
    high = values.astype(jnp.bfloat16)
    return high, (values - high.astype(jnp.float32)).astype(jnp.bfloat16)


def peer_offsets(nx, ny):
    offsets = [(a, b) for a in range(nx) for b in range(ny) if a or b]
    return sorted(offsets, key=lambda o: abs(o[1] - ny // 2))


def for_each_peer(nx, ny, ix, iy, action):
    if nx * ny <= 64:
        for a, b in peer_offsets(nx, ny):
            action(lax.rem(ix + a, nx), lax.rem(iy + b, ny))
        return

    def step(offset, carry):
        action(lax.rem(ix + offset // ny, nx), lax.rem(iy + offset % ny, ny))
        return carry

    lax.fori_loop(1, nx * ny, step, 0)


def column_reaches(ny):
    reaches = [2]
    while 2 * reaches[-1] < ny - 1:
        reaches.append(2 * reaches[-1])
    return reaches


def greet_column(ny, ix, iy, semaphore, reach):
    for step in (reach, -reach):
        there = iy + step

        @pl.when((there >= 0) & (there < ny))
        def _():
            pl.semaphore_signal(semaphore, inc=1, device_id=(ix, there), device_id_type=MESH)

    return jnp.where(iy + reach < ny, 1, 0) + jnp.where(iy >= reach, 1, 0)


def greet_row(nx, ix, iy, semaphore):
    for step in range(1, nx):
        there = lax.rem(ix + step, nx)
        pl.semaphore_signal(semaphore, inc=1, device_id=(there, iy), device_id_type=MESH)
    return nx - 1


def kernel(
    nx, ny, modes_count,
    loads_h, guess_h, inverse_h, diag_h, coup_h, rows_h, owned_h, modes_h, cinv_h,
    total, lift, stack_out,
    loads, guess, inverse, diag, coup, rows, owned, modes, cinv,
    halo_send, halo_recv, place, base, gathered, coarse_send, spread,
    in_sem, halo_ssem, halo_rsem, coarse_ssem, coarse_rsem, ready,
):
    n = nx * ny
    m, k = guess.shape
    chunks = m // LANES
    ix, iy = lax.axis_index("gx"), lax.axis_index("gy")
    me = ix * ny + iy

    pairs = [
        (rows_h, rows), (guess_h, guess), (coup_h, coup), (modes_h, modes),
        (diag_h, diag), (loads_h, loads), (cinv_h, cinv), (owned_h, owned),
        (inverse_h, inverse),
    ]
    fetch = [pltpu.make_async_copy(a, b, in_sem.at[i]) for i, (a, b) in enumerate(pairs)]
    for copy in fetch:
        copy.start()
    barrier = pltpu.get_barrier_semaphore()
    greeted = greet_row(nx, ix, iy, barrier)
    greeted += greet_column(ny, ix, iy, barrier, 1) + greet_column(ny, ix, iy, barrier, 2)

    fetch[0].wait()
    fetch[1].wait()
    guess_half = guess[...].astype(jnp.bfloat16)
    row_columns = rows[...].astype(jnp.float32).T
    lane = lax.broadcasted_iota(jnp.int32, (LANES, m), 1).astype(jnp.float32)
    for side in range(4):
        pick = one_hot(lane == row_columns[:, side : side + 1])
        values = jnp.dot(pick, guess_half, preferred_element_type=jnp.float32)
        halo_send[side] = values.astype(jnp.bfloat16)
    for side, edge in enumerate((ix == 0, ix == nx - 1, iy == 0, iy == ny - 1)):
        @pl.when(edge)
        def _():
            halo_recv[side] = jnp.zeros((LANES, k), jnp.bfloat16)

    pl.semaphore_wait(barrier, greeted)

    sends = []
    for source, target, exists, dx, dy in (
        (3, 2, iy < ny - 1, 0, 1),
        (2, 3, iy > 0, 0, -1),
        (1, 0, ix < nx - 1, 1, 0),
        (0, 1, ix > 0, -1, 0),
    ):
        copy = pltpu.make_async_remote_copy(
            src_ref=halo_send.at[source],
            dst_ref=halo_recv.at[target],
            send_sem=halo_ssem.at[source],
            recv_sem=halo_rsem.at[target],
            device_id=(ix + dx, iy + dy),
            device_id_type=MESH,
        )
        sends.append((copy, exists))
        pl.when(exists)(copy.start)
    reaches = column_reaches(ny)
    expected = greet_column(ny, ix, iy, ready.at[0], reaches[0])

    row_lanes = jnp.concatenate([rows[s : s + 1, :] for s in range(4)], axis=1)
    for j in range(chunks):
        sub = lax.broadcasted_iota(jnp.int32, (LANES, 4 * LANES), 0) + j * LANES
        place[j * LANES : (j + 1) * LANES, :] = one_hot(sub == row_lanes)
    fetch[2].wait()
    fetch[3].wait()
    zero_rows = jnp.zeros((SLOT - modes_count, LANES), jnp.float32)
    mode_rows = [
        jnp.concatenate([modes[c, :, j * LANES : (j + 1) * LANES] for c in range(modes_count)] + [zero_rows], axis=0)
        for j in range(chunks)
    ]
    scaled = jnp.concatenate([mode_rows[j] * coup[j : j + 1, :] for j in range(chunks)], axis=1)
    scaled = jnp.concatenate(split(scaled), axis=0)
    coarse_pick = jnp.dot(scaled, place[...], preferred_element_type=jnp.float32).astype(jnp.bfloat16)

    def late_base():
        fetch[4].wait()
        fetch[5].wait()
        diag_columns = diag[...].T
        for j in range(chunks):
            at = pl.ds(j * LANES, LANES)
            base[at, :] = loads[at, :].astype(jnp.float32) - diag_columns[:, j : j + 1] * guess[at, :]

    for step, reach in enumerate(reaches):
        pl.semaphore_wait(ready.at[step], expected)
        if step + 1 < len(reaches):
            expected = greet_column(ny, ix, iy, ready.at[step + 1], reaches[step + 1])
        if step == 0:
            late_base()
    expected = greet_row(nx, ix, iy, ready.at[len(reaches)])
    coarse_base = jnp.dot(
        jnp.concatenate(mode_rows, axis=1), base[...],
        precision=lax.Precision.HIGHEST, preferred_element_type=jnp.float32,
    )

    fetch[6].wait()
    group = min(n, 64)
    narrow, wide = group * modes_count, group * SLOT
    wide_at = lax.broadcasted_iota(jnp.int32, (narrow, wide), 1)
    slot_row = lax.rem(wide_at, SLOT)
    source_row = lax.div(wide_at, SLOT) * modes_count + slot_row
    narrow_at = lax.broadcasted_iota(jnp.int32, (narrow, wide), 0)
    expand = one_hot((narrow_at == source_row) & (slot_row < modes_count))
    for g in range(n // group):
        spread[:, g * wide : (g + 1) * wide] = jnp.dot(
            cinv[:, g * narrow : (g + 1) * narrow], expand, preferred_element_type=jnp.float32
        ).astype(jnp.bfloat16)
    for j in range(chunks):
        high, low = split(mode_rows[j])
        high, low = high.astype(jnp.float32), low.astype(jnp.float32)
        stack = jnp.concatenate(
            [high, high, low, jnp.zeros((LANES - 3 * SLOT, LANES), jnp.float32)], axis=0
        )
        lift[j * LANES : (j + 1) * LANES, :] = stack.T.astype(jnp.bfloat16)

    pl.semaphore_wait(ready.at[len(reaches)], expected)
    for side, exists in enumerate((ix > 0, ix < nx - 1, iy > 0, iy < ny - 1)):
        slot = halo_recv.at[side]
        arrival = pltpu.make_async_copy(slot, slot, halo_rsem.at[side])
        pl.when(exists)(arrival.wait)

    received = halo_recv[...].reshape(4 * LANES, k)
    terms = jnp.dot(coarse_pick, received, preferred_element_type=jnp.float32)
    coarse = (coarse_base + terms[:SLOT] + terms[SLOT:]).astype(jnp.bfloat16)
    coarse_send[...] = coarse
    gathered[pl.ds(me, 1)] = coarse[None]

    def send_coarse(px, py):
        pltpu.make_async_remote_copy(
            src_ref=coarse_send,
            dst_ref=gathered.at[me],
            send_sem=coarse_ssem,
            recv_sem=coarse_rsem,
            device_id=(px, py),
            device_id_type=MESH,
        ).start()

    for_each_peer(nx, ny, ix, iy, send_coarse)

    coup_columns = coup[...].T
    placed = jnp.dot(place[...], received, preferred_element_type=jnp.float32)
    residual_half = []
    for j in range(chunks):
        at = slice(j * LANES, (j + 1) * LANES)
        residual_half.append(
            (base[at, :] + coup_columns[:, j : j + 1] * placed[at]).astype(jnp.bfloat16)
        )
    residual_half = jnp.concatenate(residual_half, axis=0)
    fetch[7].wait()
    fetch[8].wait()
    owned_columns = owned[...].astype(jnp.float32).T
    for j in range(chunks):
        at = slice(j * LANES, (j + 1) * LANES)
        local = jnp.dot(inverse[at, :], residual_half, preferred_element_type=jnp.float32)
        total[at, :] = guess[at, :] + owned_columns[:, j : j + 1] * local

    for copy, exists in sends:
        pl.when(exists)(copy.wait_send)
    everyone = gathered.at[pl.ds(0, n - 1)]
    pltpu.make_async_copy(everyone, everyone, coarse_ssem).wait()
    pltpu.make_async_copy(everyone, everyone, coarse_rsem).wait()

    coef = jnp.dot(
        spread[...], gathered[...].reshape(n * SLOT, k), preferred_element_type=jnp.float32
    )
    coef = jnp.concatenate([coef, jnp.zeros((SLOT - modes_count, k), jnp.float32)], axis=0)
    high, low = split(coef)
    stack_out[...] = jnp.concatenate(
        [high, low, high, jnp.zeros((LANES - 3 * SLOT, k), jnp.bfloat16)], axis=0
    )


def finish(total, lift, stack, out_h, staged, out_sem):
    chunks = total.shape[0] // LANES
    stores = []
    for j in range(chunks):
        at = pl.ds(j * LANES, LANES)
        staged[at, :] = total[at, :] + jnp.dot(
            lift[at, :], stack[...], preferred_element_type=jnp.float32
        )
        copy = pltpu.make_async_copy(staged.at[at], out_h.at[at], out_sem.at[j])
        copy.start()
        stores.append(copy)
    for copy in stores:
        copy.wait()


def body(nx, ny, *args):
    loads, guess, inverse, diag, coup, rows, owned, modes, cinv = args
    m, k = guess.shape[2:]
    modes_count = modes.shape[3]
    n = nx * ny
    chunks = m // LANES
    small = (chunks, LANES)
    operands = (
        loads[0, 0], guess[0, 0], inverse[0, 0],
        diag.reshape(small), coup.reshape(small), rows.reshape(small), owned.reshape(small),
        jnp.transpose(modes[0], (2, 0, 1)), cinv,
    )
    scratch = [pltpu.VMEM(a.shape, a.dtype) for a in operands] + [
        pltpu.VMEM((4, LANES, k), jnp.bfloat16),
        pltpu.VMEM((4, LANES, k), jnp.bfloat16),
        pltpu.VMEM((m, 4 * LANES), jnp.bfloat16),
        pltpu.VMEM((m, k), jnp.float32),
        pltpu.VMEM((n, SLOT, k), jnp.bfloat16),
        pltpu.VMEM((SLOT, k), jnp.bfloat16),
        pltpu.VMEM((modes_count, n * SLOT), jnp.bfloat16),
        pltpu.SemaphoreType.DMA((len(operands),)),
        pltpu.SemaphoreType.DMA((4,)),
        pltpu.SemaphoreType.DMA((4,)),
        pltpu.SemaphoreType.DMA,
        pltpu.SemaphoreType.DMA,
        pltpu.SemaphoreType.REGULAR((len(column_reaches(ny)) + 1,)),
    ]
    vmem = pl.BlockSpec(memory_space=pltpu.VMEM)
    anywhere = pl.BlockSpec(memory_space=pl.ANY)
    parts = pl.pallas_call(
        functools.partial(kernel, nx, ny, modes_count),
        out_shape=(
            pltpu.VMEM((m, k), jnp.float32),
            pltpu.VMEM((m, LANES), jnp.bfloat16),
            pltpu.VMEM((LANES, k), jnp.bfloat16),
        ),
        in_specs=[pl.BlockSpec(memory_space=pltpu.HBM)] * len(operands),
        out_specs=[vmem] * 3,
        scratch_shapes=scratch,
        compiler_params=pltpu.CompilerParams(
            collective_id=0, has_side_effects=True, vmem_limit_bytes=40 << 20
        ),
    )(*operands)
    result = pl.pallas_call(
        finish,
        out_shape=jax.ShapeDtypeStruct((m, k), jnp.float32),
        in_specs=[vmem] * 3,
        out_specs=anywhere,
        scratch_shapes=[pltpu.VMEM((m, k), jnp.float32), pltpu.SemaphoreType.DMA((chunks,))],
        compiler_params=pltpu.CompilerParams(vmem_limit_bytes=16 << 20),
    )(*parts)
    return result[None, None]


def solution(mesh):
    nx, ny = mesh.shape["gx"], mesh.shape["gy"]
    return jax.shard_map(
        functools.partial(body, nx, ny),
        mesh=mesh,
        in_specs=(
            P("gx", "gy", None, None),
            P("gx", "gy", None, None),
            P("gx", "gy", None, None),
            P("gx", "gy", None),
            P("gx", "gy", None),
            P("gx", "gy", None),
            P("gx", "gy", None),
            P("gx", "gy", None, None),
            P(("gx", "gy"), None),
        ),
        out_specs=P("gx", "gy", None, None),
        check_vma=False,
    )
```

```python
import functools

import jax
import jax.numpy as jnp
from jax import lax
from jax.experimental import pallas as pl
from jax.experimental.pallas import tpu as pltpu
from jax.sharding import PartitionSpec as P

MESH = pl.DeviceIdType.MESH
LANES = 128
SLOT = 8
VMEM_BYTES = 67043328


def one_hot(mask):
    return jnp.where(mask, 1.0, 0.0).astype(jnp.bfloat16)


def split(values):
    high = values.astype(jnp.bfloat16)
    return high, (values - high.astype(jnp.float32)).astype(jnp.bfloat16)


def flipped(index, bits):
    result = index
    bit = 1
    while bit <= bits:
        if bits & bit:
            result = result + bit * (1 - 2 * lax.rem(index // bit, 2))
        bit *= 2
    return result


def for_each_peer(nx, ny, ix, iy, action):
    if nx * ny <= 64 and nx & (nx - 1) == 0 and ny & (ny - 1) == 0:
        for b in reversed(range(ny)):
            py = flipped(iy, b)
            for a in reversed(range(nx)):
                if a or b:
                    action(flipped(ix, a), py)
        return

    def step(offset, carry):
        action(lax.rem(ix + offset // ny, nx), lax.rem(iy + offset % ny, ny))
        return carry

    lax.fori_loop(1, nx * ny, step, 0)


def column_reaches(ny):
    reaches = [2]
    while 2 * reaches[-1] < ny - 1:
        reaches.append(2 * reaches[-1])
    return reaches


def greet_column(ny, ix, iy, semaphore, reach):
    for step in (reach, -reach):
        there = iy + step

        @pl.when((there >= 0) & (there < ny))
        def _():
            pl.semaphore_signal(semaphore, inc=1, device_id=(ix, there), device_id_type=MESH)

    return jnp.where(iy + reach < ny, 1, 0) + jnp.where(iy >= reach, 1, 0)


def greet_row(nx, ix, iy, semaphore):
    for step in range(1, nx):
        there = lax.rem(ix + step, nx)
        pl.semaphore_signal(semaphore, inc=1, device_id=(there, iy), device_id_type=MESH)
    return nx - 1


def kernel(
    nx, ny, modes_count,
    loads_h, guess_h, inverse_h, diag_h, coup_h, rows_h, owned_h, modes_h, cinv_h,
    total, lift, stack_out,
    loads, guess, inverse, diag, coup, rows, owned, modes, cinv,
    halo_send, halo_recv, place, base, gathered, coarse_send, spread,
    in_sem, halo_ssem, halo_rsem, coarse_ssem, coarse_rsem, ready,
):
    n = nx * ny
    m, k = guess.shape
    chunks = m // LANES
    ix, iy = lax.axis_index("gx"), lax.axis_index("gy")
    me = ix * ny + iy

    pairs = [
        (rows_h, rows), (guess_h, guess), (coup_h, coup), (modes_h, modes),
        (diag_h, diag), (loads_h, loads), (cinv_h, cinv), (owned_h, owned),
        (inverse_h, inverse),
    ]
    fetch = [pltpu.make_async_copy(a, b, in_sem.at[i]) for i, (a, b) in enumerate(pairs)]
    for copy in fetch:
        copy.start()
    gathered[...] = jnp.zeros_like(gathered)
    barrier = pltpu.get_barrier_semaphore()
    greeted = greet_row(nx, ix, iy, barrier)
    greeted += greet_column(ny, ix, iy, barrier, 1) + greet_column(ny, ix, iy, barrier, 2)

    fetch[0].wait()
    fetch[1].wait()
    guess_half = guess[...].astype(jnp.bfloat16)
    row_columns = rows[...].astype(jnp.float32).T
    lane = lax.broadcasted_iota(jnp.int32, (LANES, m), 1).astype(jnp.float32)
    for side in range(4):
        pick = one_hot(lane == row_columns[:, side : side + 1])
        values = jnp.dot(pick, guess_half, preferred_element_type=jnp.float32)
        halo_send[side] = values.astype(jnp.bfloat16)
    for side, edge in enumerate((ix == 0, ix == nx - 1, iy == 0, iy == ny - 1)):
        @pl.when(edge)
        def _():
            halo_recv[side] = jnp.zeros((LANES, k), jnp.bfloat16)

    pl.semaphore_wait(barrier, greeted)

    sends = []
    for source, target, exists, dx, dy in (
        (3, 2, iy < ny - 1, 0, 1),
        (2, 3, iy > 0, 0, -1),
        (1, 0, ix < nx - 1, 1, 0),
        (0, 1, ix > 0, -1, 0),
    ):
        copy = pltpu.make_async_remote_copy(
            src_ref=halo_send.at[source],
            dst_ref=halo_recv.at[target],
            send_sem=halo_ssem.at[source],
            recv_sem=halo_rsem.at[target],
            device_id=(ix + dx, iy + dy),
            device_id_type=MESH,
        )
        sends.append((copy, exists))
        pl.when(exists)(copy.start)
    reaches = column_reaches(ny)
    expected = greet_column(ny, ix, iy, ready.at[0], reaches[0])

    row_lanes = jnp.concatenate([rows[s : s + 1, :] for s in range(4)], axis=1)
    for j in range(chunks):
        sub = lax.broadcasted_iota(jnp.int32, (LANES, 4 * LANES), 0) + j * LANES
        place[j * LANES : (j + 1) * LANES, :] = one_hot(sub == row_lanes)
    fetch[2].wait()
    fetch[3].wait()
    zero_rows = jnp.zeros((SLOT - modes_count, LANES), jnp.float32)
    mode_rows = [
        jnp.concatenate([modes[c, :, j * LANES : (j + 1) * LANES] for c in range(modes_count)] + [zero_rows], axis=0)
        for j in range(chunks)
    ]
    scaled = jnp.concatenate([mode_rows[j] * coup[j : j + 1, :] for j in range(chunks)], axis=1)
    scaled = jnp.concatenate(split(scaled), axis=0)
    coarse_pick = jnp.dot(scaled, place[...], preferred_element_type=jnp.float32).astype(jnp.bfloat16)

    def late_base():
        fetch[4].wait()
        fetch[5].wait()
        diag_columns = diag[...].T
        for j in range(chunks):
            at = pl.ds(j * LANES, LANES)
            base[at, :] = loads[at, :].astype(jnp.float32) - diag_columns[:, j : j + 1] * guess[at, :]

    for step, reach in enumerate(reaches):
        pl.semaphore_wait(ready.at[step], expected)
        if step + 1 < len(reaches):
            expected = greet_column(ny, ix, iy, ready.at[step + 1], reaches[step + 1])
        if step == 0:
            late_base()
    expected = greet_row(nx, ix, iy, ready.at[len(reaches)])
    coarse_base = jnp.dot(
        jnp.concatenate(mode_rows, axis=1), base[...],
        precision=lax.Precision.HIGHEST, preferred_element_type=jnp.float32,
    )

    fetch[6].wait()
    group = min(n, 64)
    narrow, wide = group * modes_count, group * SLOT
    wide_at = lax.broadcasted_iota(jnp.int32, (narrow, wide), 1)
    slot_row = lax.rem(wide_at, SLOT)
    source_row = lax.div(wide_at, SLOT) * modes_count + slot_row
    narrow_at = lax.broadcasted_iota(jnp.int32, (narrow, wide), 0)
    expand = one_hot((narrow_at == source_row) & (slot_row < modes_count))
    for g in range(n // group):
        spread[:, g * wide : (g + 1) * wide] = jnp.dot(
            cinv[:, g * narrow : (g + 1) * narrow], expand, preferred_element_type=jnp.float32
        ).astype(jnp.bfloat16)
    for j in range(chunks):
        high, low = split(mode_rows[j])
        high, low = high.astype(jnp.float32), low.astype(jnp.float32)
        stack = jnp.concatenate(
            [high, high, low, jnp.zeros((LANES - 3 * SLOT, LANES), jnp.float32)], axis=0
        )
        lift[j * LANES : (j + 1) * LANES, :] = stack.T.astype(jnp.bfloat16)

    pl.semaphore_wait(ready.at[len(reaches)], expected)
    for side, exists in enumerate((ix > 0, ix < nx - 1, iy > 0, iy < ny - 1)):
        slot = halo_recv.at[side]
        arrival = pltpu.make_async_copy(slot, slot, halo_rsem.at[side])
        pl.when(exists)(arrival.wait)

    received = halo_recv[...].reshape(4 * LANES, k)
    terms = jnp.dot(coarse_pick, received, preferred_element_type=jnp.float32)
    coarse = (coarse_base + terms[:SLOT] + terms[SLOT:]).astype(jnp.bfloat16)
    coarse_send[...] = coarse
    gathered[pl.ds(me, 1)] = coarse[None]

    def send_coarse(px, py):
        pltpu.make_async_remote_copy(
            src_ref=coarse_send.at[pl.ds(0, modes_count)],
            dst_ref=gathered.at[me, pl.ds(0, modes_count)],
            send_sem=coarse_ssem,
            recv_sem=coarse_rsem,
            device_id=(px, py),
            device_id_type=MESH,
        ).start()

    for_each_peer(nx, ny, ix, iy, send_coarse)

    coup_columns = coup[...].T
    placed = jnp.dot(place[...], received, preferred_element_type=jnp.float32)
    residual_half = []
    for j in range(chunks):
        at = slice(j * LANES, (j + 1) * LANES)
        residual_half.append(
            (base[at, :] + coup_columns[:, j : j + 1] * placed[at]).astype(jnp.bfloat16)
        )
    residual_half = jnp.concatenate(residual_half, axis=0)
    fetch[7].wait()
    fetch[8].wait()
    owned_columns = owned[...].astype(jnp.float32).T
    for j in range(chunks):
        at = slice(j * LANES, (j + 1) * LANES)
        local = jnp.dot(inverse[at, :], residual_half, preferred_element_type=jnp.float32)
        total[at, :] = guess[at, :] + owned_columns[:, j : j + 1] * local

    for copy, exists in sends:
        pl.when(exists)(copy.wait_send)
    everyone = gathered.at[pl.ds(0, n - 1), pl.ds(0, modes_count)]
    pltpu.make_async_copy(everyone, everyone, coarse_ssem).wait()
    pltpu.make_async_copy(everyone, everyone, coarse_rsem).wait()

    coef = jnp.dot(
        spread[...], gathered[...].reshape(n * SLOT, k), preferred_element_type=jnp.float32
    )
    coef = jnp.concatenate([coef, jnp.zeros((SLOT - modes_count, k), jnp.float32)], axis=0)
    high, low = split(coef)
    stack_out[...] = jnp.concatenate(
        [high, low, high, jnp.zeros((LANES - 3 * SLOT, k), jnp.bfloat16)], axis=0
    )


def finish(total, lift, stack, out_h, staged, out_sem):
    chunks = total.shape[0] // LANES
    stores = []
    for j in range(chunks):
        at = pl.ds(j * LANES, LANES)
        staged[at, :] = total[at, :] + jnp.dot(
            lift[at, :], stack[...], preferred_element_type=jnp.float32
        )
        copy = pltpu.make_async_copy(staged.at[at], out_h.at[at], out_sem.at[j])
        copy.start()
        stores.append(copy)
    for copy in stores:
        copy.wait()


def body(nx, ny, *args):
    loads, guess, inverse, diag, coup, rows, owned, modes, cinv = args
    m, k = guess.shape[2:]
    modes_count = modes.shape[3]
    n = nx * ny
    chunks = m // LANES
    small = (chunks, LANES)
    operands = (
        loads[0, 0], guess[0, 0], inverse[0, 0],
        diag.reshape(small), coup.reshape(small), rows.reshape(small), owned.reshape(small),
        jnp.transpose(modes[0], (2, 0, 1)), cinv,
    )
    scratch = [pltpu.VMEM(a.shape, a.dtype) for a in operands] + [
        pltpu.VMEM((4, LANES, k), jnp.bfloat16),
        pltpu.VMEM((4, LANES, k), jnp.bfloat16),
        pltpu.VMEM((m, 4 * LANES), jnp.bfloat16),
        pltpu.VMEM((m, k), jnp.float32),
        pltpu.VMEM((n, SLOT, k), jnp.bfloat16),
        pltpu.VMEM((SLOT, k), jnp.bfloat16),
        pltpu.VMEM((modes_count, n * SLOT), jnp.bfloat16),
        pltpu.SemaphoreType.DMA((len(operands),)),
        pltpu.SemaphoreType.DMA((4,)),
        pltpu.SemaphoreType.DMA((4,)),
        pltpu.SemaphoreType.DMA,
        pltpu.SemaphoreType.DMA,
        pltpu.SemaphoreType.REGULAR((len(column_reaches(ny)) + 1,)),
    ]
    kept = m * k * 4 + m * LANES * 2 + LANES * k * 2
    vmem = pl.BlockSpec(memory_space=pltpu.VMEM)
    anywhere = pl.BlockSpec(memory_space=pl.ANY)
    parts = pl.pallas_call(
        functools.partial(kernel, nx, ny, modes_count),
        out_shape=(
            pltpu.VMEM((m, k), jnp.float32),
            pltpu.VMEM((m, LANES), jnp.bfloat16),
            pltpu.VMEM((LANES, k), jnp.bfloat16),
        ),
        in_specs=[anywhere] * len(operands),
        out_specs=[vmem] * 3,
        scratch_shapes=scratch,
        compiler_params=pltpu.CompilerParams(
            collective_id=0, has_side_effects=True, vmem_limit_bytes=VMEM_BYTES - kept - (64 << 10)
        ),
    )(*operands)
    result = pl.pallas_call(
        finish,
        out_shape=jax.ShapeDtypeStruct((m, k), jnp.float32),
        in_specs=[vmem] * 3,
        out_specs=anywhere,
        scratch_shapes=[pltpu.VMEM((m, k), jnp.float32), pltpu.SemaphoreType.DMA((chunks,))],
        compiler_params=pltpu.CompilerParams(vmem_limit_bytes=16 << 20),
    )(*parts)
    return result[None, None]


def solution(mesh):
    nx, ny = mesh.shape["gx"], mesh.shape["gy"]
    return jax.shard_map(
        functools.partial(body, nx, ny),
        mesh=mesh,
        in_specs=(
            P("gx", "gy", None, None),
            P("gx", "gy", None, None),
            P("gx", "gy", None, None),
            P("gx", "gy", None),
            P("gx", "gy", None),
            P("gx", "gy", None),
            P("gx", "gy", None),
            P("gx", "gy", None, None),
            P(("gx", "gy"), None),
        ),
        out_specs=P("gx", "gy", None, None),
        check_vma=False,
    )
```

```python
import functools

import jax
import jax.numpy as jnp
from jax import lax
from jax.experimental import pallas as pl
from jax.experimental.pallas import tpu as pltpu
from jax.sharding import PartitionSpec as P

MESH = pl.DeviceIdType.MESH
LANES = 128
SLOT = 8
VMEM_BYTES = 67043328


def one_hot(mask):
    return jnp.where(mask, 1.0, 0.0).astype(jnp.bfloat16)


def split(values):
    high = values.astype(jnp.bfloat16)
    return high, (values - high.astype(jnp.float32)).astype(jnp.bfloat16)


def flipped(index, bits):
    result = index
    bit = 1
    while bit <= bits:
        if bits & bit:
            result = result + bit * (1 - 2 * lax.rem(index // bit, 2))
        bit *= 2
    return result


def for_each_peer(nx, ny, ix, iy, action):
    if nx * ny <= 64 and nx & (nx - 1) == 0 and ny & (ny - 1) == 0:
        for b in reversed(range(ny)):
            py = flipped(iy, b)
            for a in reversed(range(nx)):
                if a or b:
                    action(flipped(ix, a), py)
        return

    def step(offset, carry):
        action(lax.rem(ix + offset // ny, nx), lax.rem(iy + offset % ny, ny))
        return carry

    lax.fori_loop(1, nx * ny, step, 0)


def column_reaches(ny):
    reaches = [2]
    while 2 * reaches[-1] < ny - 1:
        reaches.append(2 * reaches[-1])
    return reaches


def greet_column(ny, ix, iy, semaphore, reach):
    for step in (reach, -reach):
        there = iy + step

        @pl.when((there >= 0) & (there < ny))
        def _():
            pl.semaphore_signal(semaphore, inc=1, device_id=(ix, there), device_id_type=MESH)

    return jnp.where(iy + reach < ny, 1, 0) + jnp.where(iy >= reach, 1, 0)


def greet_row(nx, ix, iy, semaphore):
    for step in range(1, nx):
        there = lax.rem(ix + step, nx)
        pl.semaphore_signal(semaphore, inc=1, device_id=(there, iy), device_id_type=MESH)
    return nx - 1


def kernel(
    nx, ny, modes_count,
    loads_h, guess_h, inverse_h, diag_h, coup_h, rows_h, owned_h, modes_h, cinv_h,
    total, weights, coarse_all,
    loads, guess, inverse, diag, coup, rows, owned, modes, cinv,
    halo_send, halo_recv, place, base, gathered, coarse_send,
    in_sem, halo_ssem, halo_rsem, coarse_ssem, coarse_rsem, ready,
):
    n = nx * ny
    m, k = guess.shape
    chunks = m // LANES
    ix, iy = lax.axis_index("gx"), lax.axis_index("gy")
    me = ix * ny + iy

    pairs = [
        (rows_h, rows), (guess_h, guess), (coup_h, coup), (modes_h, modes),
        (diag_h, diag), (loads_h, loads), (cinv_h, cinv), (owned_h, owned),
        (inverse_h, inverse),
    ]
    fetch = [pltpu.make_async_copy(a, b, in_sem.at[i]) for i, (a, b) in enumerate(pairs)]
    for copy in fetch:
        copy.start()
    gathered[...] = jnp.zeros_like(gathered)
    barrier = pltpu.get_barrier_semaphore()
    greeted = greet_row(nx, ix, iy, barrier)
    greeted += greet_column(ny, ix, iy, barrier, 1) + greet_column(ny, ix, iy, barrier, 2)

    fetch[0].wait()
    fetch[1].wait()
    guess_half = guess[...].astype(jnp.bfloat16)
    row_columns = rows[...].astype(jnp.float32).T
    lane = lax.broadcasted_iota(jnp.int32, (LANES, m), 1).astype(jnp.float32)
    for side in range(4):
        pick = one_hot(lane == row_columns[:, side : side + 1])
        values = jnp.dot(pick, guess_half, preferred_element_type=jnp.float32)
        halo_send[side] = values.astype(jnp.bfloat16)
    for side, edge in enumerate((ix == 0, ix == nx - 1, iy == 0, iy == ny - 1)):
        @pl.when(edge)
        def _():
            halo_recv[side] = jnp.zeros((LANES, k), jnp.bfloat16)

    pl.semaphore_wait(barrier, greeted)

    sends = []
    for source, target, exists, dx, dy in (
        (3, 2, iy < ny - 1, 0, 1),
        (2, 3, iy > 0, 0, -1),
        (1, 0, ix < nx - 1, 1, 0),
        (0, 1, ix > 0, -1, 0),
    ):
        copy = pltpu.make_async_remote_copy(
            src_ref=halo_send.at[source],
            dst_ref=halo_recv.at[target],
            send_sem=halo_ssem.at[source],
            recv_sem=halo_rsem.at[target],
            device_id=(ix + dx, iy + dy),
            device_id_type=MESH,
        )
        sends.append((copy, exists))
        pl.when(exists)(copy.start)
    reaches = column_reaches(ny)
    expected = greet_column(ny, ix, iy, ready.at[0], reaches[0])

    row_lanes = jnp.concatenate([rows[s : s + 1, :] for s in range(4)], axis=1)
    for j in range(chunks):
        sub = lax.broadcasted_iota(jnp.int32, (LANES, 4 * LANES), 0) + j * LANES
        place[j * LANES : (j + 1) * LANES, :] = one_hot(sub == row_lanes)
    fetch[2].wait()
    fetch[3].wait()
    zero_rows = jnp.zeros((SLOT - modes_count, LANES), jnp.float32)
    mode_rows = [
        jnp.concatenate([modes[c, :, j * LANES : (j + 1) * LANES] for c in range(modes_count)] + [zero_rows], axis=0)
        for j in range(chunks)
    ]
    scaled = jnp.concatenate([mode_rows[j] * coup[j : j + 1, :] for j in range(chunks)], axis=1)
    scaled = jnp.concatenate(split(scaled), axis=0)
    coarse_pick = jnp.dot(scaled, place[...], preferred_element_type=jnp.float32).astype(jnp.bfloat16)

    def late_base():
        fetch[4].wait()
        fetch[5].wait()
        diag_columns = diag[...].T
        for j in range(chunks):
            at = pl.ds(j * LANES, LANES)
            base[at, :] = loads[at, :].astype(jnp.float32) - diag_columns[:, j : j + 1] * guess[at, :]

    for step, reach in enumerate(reaches):
        pl.semaphore_wait(ready.at[step], expected)
        if step + 1 < len(reaches):
            expected = greet_column(ny, ix, iy, ready.at[step + 1], reaches[step + 1])
        if step == 0:
            late_base()
    expected = greet_row(nx, ix, iy, ready.at[len(reaches)])
    coarse_base = jnp.dot(
        jnp.concatenate(mode_rows, axis=1), base[...],
        precision=lax.Precision.HIGHEST, preferred_element_type=jnp.float32,
    )

    pl.semaphore_wait(ready.at[len(reaches)], expected)
    for side, exists in enumerate((ix > 0, ix < nx - 1, iy > 0, iy < ny - 1)):
        slot = halo_recv.at[side]
        arrival = pltpu.make_async_copy(slot, slot, halo_rsem.at[side])
        pl.when(exists)(arrival.wait)

    received = halo_recv[...].reshape(4 * LANES, k)
    terms = jnp.dot(coarse_pick, received, preferred_element_type=jnp.float32)
    coarse = (coarse_base + terms[:SLOT] + terms[SLOT:]).astype(jnp.bfloat16)
    coarse_send[...] = coarse
    gathered[pl.ds(me, 1)] = coarse[None]

    def send_coarse(px, py):
        pltpu.make_async_remote_copy(
            src_ref=coarse_send.at[pl.ds(0, modes_count)],
            dst_ref=gathered.at[me, pl.ds(0, modes_count)],
            send_sem=coarse_ssem,
            recv_sem=coarse_rsem,
            device_id=(px, py),
            device_id_type=MESH,
        ).start()

    for_each_peer(nx, ny, ix, iy, send_coarse)

    fetch[6].wait()
    group = min(n, 64)
    narrow, wide = group * modes_count, group * SLOT
    wide_at = lax.broadcasted_iota(jnp.int32, (narrow, wide), 1)
    slot_row = lax.rem(wide_at, SLOT)
    source_row = lax.div(wide_at, SLOT) * modes_count + slot_row
    narrow_at = lax.broadcasted_iota(jnp.int32, (narrow, wide), 0)
    expand = one_hot((narrow_at == source_row) & (slot_row < modes_count))
    lifts = []
    for j in range(chunks):
        high, low = split(mode_rows[j])
        high, low = high.astype(jnp.float32), low.astype(jnp.float32)
        stack = jnp.concatenate(
            [high, low, jnp.zeros((LANES - 2 * SLOT, LANES), jnp.float32)], axis=0
        )
        lifts.append(stack.T.astype(jnp.bfloat16))
    pad = jnp.zeros((SLOT - modes_count, wide), jnp.float32)
    rest = jnp.zeros((LANES - 2 * SLOT, wide), jnp.float32)
    for g in range(n // group):
        spread = jnp.dot(
            cinv[:, g * narrow : (g + 1) * narrow], expand, preferred_element_type=jnp.float32
        )
        stack = jnp.concatenate([spread, pad, spread, pad, rest], axis=0).astype(jnp.bfloat16)
        for j in range(chunks):
            weights[j * LANES : (j + 1) * LANES, g * wide : (g + 1) * wide] = jnp.dot(
                lifts[j], stack, preferred_element_type=jnp.float32
            ).astype(jnp.bfloat16)
    coup_columns = coup[...].T
    placed = jnp.dot(place[...], received, preferred_element_type=jnp.float32)
    residual_half = []
    for j in range(chunks):
        at = slice(j * LANES, (j + 1) * LANES)
        residual_half.append(
            (base[at, :] + coup_columns[:, j : j + 1] * placed[at]).astype(jnp.bfloat16)
        )
    residual_half = jnp.concatenate(residual_half, axis=0)
    fetch[7].wait()
    fetch[8].wait()
    owned_columns = owned[...].astype(jnp.float32).T
    for j in range(chunks):
        at = slice(j * LANES, (j + 1) * LANES)
        local = jnp.dot(inverse[at, :], residual_half, preferred_element_type=jnp.float32)
        total[at, :] = guess[at, :] + owned_columns[:, j : j + 1] * local

    for copy, exists in sends:
        pl.when(exists)(copy.wait_send)
    everyone = gathered.at[pl.ds(0, n - 1), pl.ds(0, modes_count)]
    pltpu.make_async_copy(everyone, everyone, coarse_ssem).wait()
    pltpu.make_async_copy(everyone, everyone, coarse_rsem).wait()

    coarse_all[...] = gathered[...].reshape(n * SLOT, k)


def finish(total, weights, coarse_all, out_h, staged, out_sem):
    chunks = total.shape[0] // LANES
    stores = []
    for j in range(chunks):
        at = pl.ds(j * LANES, LANES)
        staged[at, :] = total[at, :] + jnp.dot(
            weights[at, :], coarse_all[...], preferred_element_type=jnp.float32
        )
        copy = pltpu.make_async_copy(staged.at[at], out_h.at[at], out_sem.at[j])
        copy.start()
        stores.append(copy)
    for copy in stores:
        copy.wait()


def body(nx, ny, *args):
    loads, guess, inverse, diag, coup, rows, owned, modes, cinv = args
    m, k = guess.shape[2:]
    modes_count = modes.shape[3]
    n = nx * ny
    chunks = m // LANES
    small = (chunks, LANES)
    operands = (
        loads[0, 0], guess[0, 0], inverse[0, 0],
        diag.reshape(small), coup.reshape(small), rows.reshape(small), owned.reshape(small),
        jnp.transpose(modes[0], (2, 0, 1)), cinv,
    )
    scratch = [pltpu.VMEM(a.shape, a.dtype) for a in operands] + [
        pltpu.VMEM((4, LANES, k), jnp.bfloat16),
        pltpu.VMEM((4, LANES, k), jnp.bfloat16),
        pltpu.VMEM((m, 4 * LANES), jnp.bfloat16),
        pltpu.VMEM((m, k), jnp.float32),
        pltpu.VMEM((n, SLOT, k), jnp.bfloat16),
        pltpu.VMEM((SLOT, k), jnp.bfloat16),
        pltpu.SemaphoreType.DMA((len(operands),)),
        pltpu.SemaphoreType.DMA((4,)),
        pltpu.SemaphoreType.DMA((4,)),
        pltpu.SemaphoreType.DMA,
        pltpu.SemaphoreType.DMA,
        pltpu.SemaphoreType.REGULAR((len(column_reaches(ny)) + 1,)),
    ]
    kept = m * k * 4 + (m + k) * n * SLOT * 2
    vmem = pl.BlockSpec(memory_space=pltpu.VMEM)
    anywhere = pl.BlockSpec(memory_space=pl.ANY)
    parts = pl.pallas_call(
        functools.partial(kernel, nx, ny, modes_count),
        out_shape=(
            pltpu.VMEM((m, k), jnp.float32),
            pltpu.VMEM((m, n * SLOT), jnp.bfloat16),
            pltpu.VMEM((n * SLOT, k), jnp.bfloat16),
        ),
        in_specs=[anywhere] * len(operands),
        out_specs=[vmem] * 3,
        scratch_shapes=scratch,
        compiler_params=pltpu.CompilerParams(
            collective_id=0, has_side_effects=True, vmem_limit_bytes=VMEM_BYTES - kept - (64 << 10)
        ),
    )(*operands)
    result = pl.pallas_call(
        finish,
        out_shape=jax.ShapeDtypeStruct((m, k), jnp.float32),
        in_specs=[vmem] * 3,
        out_specs=anywhere,
        scratch_shapes=[pltpu.VMEM((m, k), jnp.float32), pltpu.SemaphoreType.DMA((chunks,))],
        compiler_params=pltpu.CompilerParams(vmem_limit_bytes=16 << 20),
    )(*parts)
    return result[None, None]


def solution(mesh):
    nx, ny = mesh.shape["gx"], mesh.shape["gy"]
    return jax.shard_map(
        functools.partial(body, nx, ny),
        mesh=mesh,
        in_specs=(
            P("gx", "gy", None, None),
            P("gx", "gy", None, None),
            P("gx", "gy", None, None),
            P("gx", "gy", None),
            P("gx", "gy", None),
            P("gx", "gy", None),
            P("gx", "gy", None),
            P("gx", "gy", None, None),
            P(("gx", "gy"), None),
        ),
        out_specs=P("gx", "gy", None, None),
        check_vma=False,
    )
```
